128 devices in a mesh: shot: 4 (over y_hi, core), slab: 32 (over z, x, y_lo).
Axes of the slice: x: 4, y: 4 (y_hi: 2, y_lo: 2; y = y_hi * 2 + y_lo), z: 4, core: 2. Of those that a mesh axis runs over, the one named last changes fastest.
Arguments:
- source_field: bfloat16 [12, 8, 128, 256, 128], P('shot', None, 'slab'), may hold values from -4 to 4
- receiver_field: bfloat16 [12, 8, 128, 256, 128], P('shot', None, 'slab'), may hold values from -4 to 4
- shot_group: int32 [12], replicated, may hold values from 0 to 11
- first_weight: bfloat16 [32, 12, 3, 3, 3], replicated, may hold values from -0.3125 to 0.3125
- first_bias: float32 [32], replicated, may hold values from -3 to 3
- second_weight: bfloat16 [32, 32, 3, 3, 3], replicated, may hold values from -0.21875 to 0.21875
- second_bias: float32 [32], replicated, may hold values from -3 to 3
Outputs:
- features: bfloat16 [32, 128, 256, 128], P(None, 'shot', 'slab')
The draws below stay inside these ranges and needn't reach their ends.
All inputs are finite; a program needn't handle non-finite values.
Results may differ from the reference program's by a relative error of at most 0.01.
Values may be sent and summed in bfloat16 or wider, within the bound.
No kernel may reach another device: no remote copies, remote signals or barrier semaphores. Data moves between devices by JAX's collectives and lax.ppermute only.
A program may use at most 128 MiB of HBM per device.

```python
import math
import jax
import jax.numpy as jnp
from jax import lax

GROUPS = 12
CH = 32
TSTEPS = 8
NX = 256
NY = 128
SHOTS = 12
NZ = 128


def touch_ends(drawn, rng, smallest, high):
    spot = [jax.random.randint(jax.random.fold_in(rng, axis), (), 0, length) for axis, length in enumerate(drawn.shape)]
    longest = drawn.shape.index(max(drawn.shape))
    neighbour = spot[:longest] + [(spot[longest] + 1) % drawn.shape[longest]] + spot[longest + 1:]
    return drawn.at[tuple(spot)].set(smallest).at[tuple(neighbour)].set(high)


def steps_of(rng, shape, split, least, high):
    loudness = 1.0
    for dim, shards_of in split:
        steps = jax.random.uniform(jax.random.fold_in(jax.random.fold_in(rng, 6), dim), (shards_of,), jnp.float32, least / len(split), high / len(split))
        loudness = loudness * jnp.repeat(jnp.exp(steps), shape[dim] // shards_of).reshape((-1,) + (1,) * (len(shape) - 1 - dim))
    return loudness


def normal_values(stream_key, extent, scale, limit, shards=(), kind=jnp.bfloat16):
    values = scale * jax.random.normal(stream_key, extent, jnp.float32)
    if shards:
        values = values * steps_of(stream_key, extent, shards, -0.22, 0.18)
    return jnp.clip(values, -limit, limit).astype(kind)


def setup_inputs(seed: int = 0) -> dict:
    seeds = jax.random.split(jax.random.key(seed), 8)
    return {
        "source_field": normal_values(seeds[0], (SHOTS, TSTEPS, NZ, NX, NY), 0.6, 4.0, ((0, 4), (2, 32))),
        "receiver_field": normal_values(seeds[1], (SHOTS, TSTEPS, NZ, NX, NY), 0.6, 4.0, ((0, 4), (2, 32))),
        "shot_group": touch_ends(jax.random.randint(seeds[2], (SHOTS,), 0, GROUPS), jax.random.fold_in(seeds[2], 1), 0, GROUPS - 1).astype(jnp.int32),
        "first_weight": normal_values(seeds[3], (CH, GROUPS, 3, 3, 3), (GROUPS * 27) ** -0.5, 0.3125),
        "first_bias": normal_values(seeds[4], (CH,), 0.5, 3.0, (), jnp.float32),
        "second_weight": normal_values(seeds[5], (CH, CH, 3, 3, 3), (CH * 27) ** -0.5, 0.21875),
        "second_bias": normal_values(seeds[6], (CH,), 0.5, 3.0, (), jnp.float32),
    }


def convolve_blocks(field, weight, biases):
    channels, extent_z, extent_x, extent_y = field.shape
    block_span = math.gcd(extent_z, 32)
    padded = jnp.pad(field.astype(jnp.float32), ((0, 0), (1, 1), (1, 1), (0, 0)))
    weight_wide = weight.astype(jnp.float32)

    def one_block(block_index):
        start = (block_index * block_span).astype(jnp.int32)
        window = lax.dynamic_slice(padded, (jnp.int32(0), start, jnp.int32(0), jnp.int32(0)), (channels, block_span + 2, extent_x + 2, extent_y))
        result = lax.conv_general_dilated(window[None], weight_wide, (1, 1, 1), ((0, 0), (0, 0), (1, 1)), dimension_numbers=("NCDHW", "OIDHW", "NCDHW"), precision=lax.Precision.HIGHEST)[0]
        return jnp.maximum(result + biases[:, None, None, None], 0.0).astype(jnp.bfloat16)

    blocks = lax.map(one_block, jnp.arange(extent_z // block_span, dtype=jnp.int32))
    return jnp.moveaxis(blocks, 0, 1).reshape(weight.shape[0], extent_z, extent_x, extent_y)


def reference(source_field, receiver_field, shot_group, first_weight, first_bias, second_weight, second_bias):
    total_shots = source_field.shape[0]
    labels = jnp.arange(GROUPS, dtype=jnp.int32)
    image_sum = jnp.zeros((GROUPS,) + source_field.shape[2:], jnp.float32)
    for shot_index in range(total_shots):
        cross_term = jnp.einsum("tzxy,tzxy->zxy", source_field[shot_index].astype(jnp.float32), receiver_field[shot_index].astype(jnp.float32))
        member = (labels == shot_group[shot_index]).astype(jnp.float32)
        image_sum = image_sum + member[:, None, None, None] * cross_term[None]
    image_tile = image_sum.astype(jnp.bfloat16)
    hidden = convolve_blocks(image_tile, first_weight, first_bias)
    return convolve_blocks(hidden, second_weight, second_bias)
```

```python
import functools

import jax
import jax.numpy as jnp
from jax import lax
from jax.experimental import pallas as pl
from jax.experimental.pallas import tpu as pltpu
from jax.sharding import PartitionSpec as P

SC = 16

def cross_kernel(src_ref, rec_ref, out_ref, wide_ref):
    planes, nx, ny = src_ref.shape[2:]
    first = (pl.program_id(0) == 0) & (pl.program_id(1) == 0)
    edge = 2 * planes
    @pl.when(first)
    def _():
        wide_ref[0:edge, :] = jnp.zeros((edge, ny), jnp.float32)
        wide_ref[edge + planes * nx :, :] = jnp.zeros((edge, ny), jnp.float32)
    for z in range(planes):
        total = jnp.zeros((nx, ny), jnp.float32)
        for t in range(src_ref.shape[1]):
            total = total + src_ref[0, t, z].astype(jnp.float32) * rec_ref[0, t, z].astype(jnp.float32)
        wide_ref[pl.ds(edge + z, nx, stride=planes), :] = total
    rows = out_ref.shape[3]
    step = rows - 2 * edge
    for d in range(out_ref.shape[0]):
        out_ref[d, 0, 0] = wide_ref[d * step : d * step + rows, :].astype(out_ref.dtype)

def cross_pieces(source, receiver, targets):
    shots, steps, planes, nx, ny = source.shape
    halves = 2
    p = planes // halves
    rows = (nx // targets + 4) * p
    spec = pl.BlockSpec((1, steps, p, nx, ny), lambda s, h: (s, 0, h, 0, 0))
    return pl.pallas_call(
        cross_kernel,
        grid=(shots, halves),
        in_specs=[spec, spec],
        out_specs=pl.BlockSpec((targets, 1, 1, rows, ny), lambda s, h: (0, h, s, 0, 0)),
        out_shape=jax.ShapeDtypeStruct((targets, halves, shots, rows, ny), jnp.bfloat16),
        scratch_shapes=[pltpu.VMEM(((nx + 4) * p, ny), jnp.float32)],
        compiler_params=pltpu.CompilerParams(vmem_limit_bytes=48 << 20),
        name="cross",
    )(source, receiver)

def spread(part, bias):
    co = bias.shape[0]
    ny = part.shape[1]
    lane = lax.broadcasted_iota(jnp.int32, (co, ny), 1)
    low = jnp.where(lane == 0, 0.0, pltpu.roll(part[:co], 1, 1))
    high = jnp.where(lane == ny - 1, 0.0, pltpu.roll(part[2 * co :], ny - 1, 1))
    return jnp.maximum(part[co : 2 * co] + low + high + bias, 0.0)

def conv_kernel(place, group_ref, p0, p1, p2, p3, w1_ref, b1_ref, w2_ref, b2_ref,
                out_ref, x_ref, h_ref, gather_ref, k1_ref, k2_ref, bias_ref, turn_ref):
    co, ci = w1_ref.shape[1:]
    ny = x_ref.shape[-1]
    nhx = h_ref.shape[1]
    nox = out_ref.shape[2]
    nh = p0.shape[0]
    rows = p0.shape[2]
    shots = p0.shape[1]
    per = 2
    step = pl.program_id(0)
    zs = out_ref.shape[1]
    i, ni, j, nj = place()

    def hidden_row(z, live=None):
        for x in range(0, nhx, 2):
            right = jnp.concatenate(
                [jnp.concatenate([x_ref[z + dz, x + q + dx] for dz in range(3) for dx in range(3)], axis=0) for q in range(2)], axis=1)
            part = jnp.dot(k1_ref[...], right, preferred_element_type=jnp.float32)
            for q in range(2):
                v = spread(part[:, q * ny : (q + 1) * ny], bias_ref[0])
                if x + q == 0:
                    v = jnp.where(j > 0, v, 0.0)
                if x + q == nhx - 1:
                    v = jnp.where(j < nj - 1, v, 0.0)
                if live is not None:
                    v = jnp.where(live, v, 0.0)
                h_ref[z, x + q] = v.astype(h_ref.dtype)

    @pl.when(step == 0)
    def _():
        taps = 9
        w = k1_ref.shape[1]
        r = lax.broadcasted_iota(jnp.int32, (ci, w), 0)
        c = lax.broadcasted_iota(jnp.int32, (ci, w), 1)
        label = jnp.full((ci, w), -1, jnp.int32)
        for k in range(4):
            for s in range(shots):
                label = jnp.where(c % SC == k * shots + s, group_ref[(i ^ k) * shots + s], label)
        hit = r == label
        acc = jnp.zeros((3 * co, w), jnp.float32)
        for t in range(taps):
            pick = jnp.where(hit & (c // SC == t), 1.0, 0.0).astype(jnp.bfloat16)
            left = jnp.concatenate([w1_ref[3 * t + dy] for dy in range(3)], axis=0)
            acc = acc + jnp.dot(left, pick, preferred_element_type=jnp.float32)
            for dy in range(3):
                k2_ref[dy * co : (dy + 1) * co, t * co : (t + 1) * co] = w2_ref[3 * t + dy]
        k1_ref[...] = acc.astype(jnp.bfloat16)
        eye = lax.broadcasted_iota(jnp.int32, (co, co), 0) == lax.broadcasted_iota(jnp.int32, (co, co), 1)
        for n, b in enumerate((b1_ref, b2_ref)):
            col = jnp.sum(jnp.where(eye, jnp.broadcast_to(b[...], (co, co)), 0.0), axis=1, keepdims=True)
            bias_ref[n] = jnp.broadcast_to(col, (co, ny))
        gather_ref[...] = jnp.zeros(gather_ref.shape, jnp.float32)

        @pl.loop(0, nh)
        def _(l):
            want = l + jnp.where(i == 0, -1, jnp.where(i == ni - 1, 1, 0))
            here = jnp.clip(want, 0, nh - 1)
            keep = jnp.where(want == here, 1.0, 0.0)
            for k, p in enumerate((p0, p1, p2, p3)):
                for s in range(shots):
                    gather_ref[pl.ds(k * shots + s, rows, stride=SC), :] = p[here, s].astype(jnp.float32) * keep
            for x in range(rows // per):
                for z in range(per):
                    at = (x * per + z) * SC
                    x_ref[l * per + z, x] = gather_ref[at : at + SC, :].astype(jnp.bfloat16)

        for z in range(3):
            hidden_row(z)

        @pl.when(i == 0)
        def _():
            h_ref[0] = jnp.zeros(h_ref.shape[1:], h_ref.dtype)

    @pl.when(step == pl.num_programs(0))
    def _():
        out_ref[0, 0] = h_ref[step, 0, 0:8, :].astype(out_ref.dtype)
    @pl.loop(0, zs)
    def _(k):
        z = step * zs + k
        for x in range(0, nox, 2):
            right = jnp.concatenate(
                [jnp.concatenate([h_ref[z + dz, x + q + dx] for dz in range(3) for dx in range(3)], axis=0) for q in range(2)], axis=1)
            part = jnp.dot(k2_ref[...], right, preferred_element_type=jnp.float32)
            for q in range(2):
                turn_ref[pl.ds(x + q, co, stride=nox), :] = spread(part[:, q * ny : (q + 1) * ny], bias_ref[1])
        out_ref[:, k] = turn_ref[...].reshape(co, nox, ny).astype(out_ref.dtype)
        hidden_row(z + 3, (z != h_ref.shape[0] - 5) | (i < ni - 1))

def convolutions(place, shot_group, pieces, w1, b1, w2, b2, zs=4):
    nh, shots, rows, ny = pieces[0].shape
    nz = nh * 2 - 4
    nx = rows // 2 - 4
    co = w1.shape[0]
    ci = w1.shape[1]
    w1t = w1.transpose(2, 3, 4, 0, 1).reshape(27, co, ci)
    w2t = w2.transpose(2, 3, 4, 0, 1).reshape(27, co, co)
    whole = lambda a: pl.BlockSpec(a.shape, lambda s: (0,) * a.ndim)
    b1 = b1.reshape(1, co); b2 = b2.reshape(1, co)
    vm = [*pieces, w1t, b1, w2t, b2]
    return pl.pallas_call(
        functools.partial(conv_kernel, place),
        grid=(nz // zs,),
        in_specs=[pl.BlockSpec(memory_space=pltpu.SMEM)] + [whole(a) for a in vm],
        out_specs=pl.BlockSpec((co, zs, nx, ny), lambda s: (0, s, 0, 0)),
        out_shape=jax.ShapeDtypeStruct((co, nz, nx, ny), jnp.bfloat16),
        scratch_shapes=[
            pltpu.VMEM((nz + 5, nx + 4, SC, ny), jnp.bfloat16),
            pltpu.VMEM((nz + 3, nx + 2, co, ny), jnp.bfloat16),
            pltpu.VMEM((rows * SC, ny), jnp.float32),
            pltpu.VMEM((3 * co, 9 * SC), jnp.bfloat16),
            pltpu.VMEM((3 * co, 9 * co), jnp.bfloat16),
            pltpu.VMEM((2, co, ny), jnp.float32),
            pltpu.VMEM((nx * co, ny), jnp.float32),
        ],
        compiler_params=pltpu.CompilerParams(vmem_limit_bytes=48 << 20),
        name="convolutions",
    )(shot_group, *vm)


def shards(source, receiver, shot_group, w1, b1, w2, b2):
    ni, nj = lax.axis_size("shot"), lax.axis_size("slab")
    i = lax.axis_index("shot")
    pieces = cross_pieces(source, receiver, nj)
    swapped = lax.all_to_all(pieces, "slab", 0, 0, tiled=True)
    halves = swapped.reshape((-1,) + swapped.shape[2:])
    span = halves.shape[0] // ni
    here = []
    for k in range(ni):
        start = jnp.clip((i ^ k) * span - 1, 0, halves.shape[0] - span - 2)
        part = lax.dynamic_slice_in_dim(halves, start, span + 2, 0)
        here.append(part if k == 0 else lax.ppermute(part, "shot", [(a, a ^ k) for a in range(ni)]))
    place = lambda: (lax.axis_index("shot"), ni, lax.axis_index("slab"), nj)
    return convolutions(place, shot_group, here, w1, b1, w2, b2)


def solution(mesh):
    fields = P("shot", None, "slab", None, None)
    return jax.shard_map(
        shards, mesh=mesh, in_specs=(fields, fields, P(), P(), P(), P(), P()),
        out_specs=P(None, "shot", "slab", None), check_vma=False)
```

```python
import functools

import jax
import jax.numpy as jnp
from jax import lax
from jax.experimental import pallas as pl
from jax.experimental.pallas import tpu as pltpu
from jax.sharding import PartitionSpec as P

SC = 16

def cross_kernel(src_ref, rec_ref, out_ref, wide_ref):
    planes, nx, ny = src_ref.shape[2:]
    first = (pl.program_id(0) == 0) & (pl.program_id(1) == 0)
    edge = 2 * planes
    @pl.when(first)
    def _():
        wide_ref[0:edge, :] = jnp.zeros((edge, ny), jnp.float32)
        wide_ref[edge + planes * nx :, :] = jnp.zeros((edge, ny), jnp.float32)
    for z in range(planes):
        total = jnp.zeros((nx, ny), jnp.float32)
        for t in range(src_ref.shape[1]):
            total = total + src_ref[0, t, z].astype(jnp.float32) * rec_ref[0, t, z].astype(jnp.float32)
        wide_ref[pl.ds(edge + z, nx, stride=planes), :] = total
    rows = out_ref.shape[3]
    step = rows - 2 * edge
    for d in range(out_ref.shape[0]):
        out_ref[d, 0, 0] = wide_ref[d * step : d * step + rows, :].astype(out_ref.dtype)

def cross_pieces(source, receiver, targets):
    shots, steps, planes, nx, ny = source.shape
    halves = 2
    p = planes // halves
    rows = (nx // targets + 4) * p
    spec = pl.BlockSpec((1, steps, p, nx, ny), lambda s, h: (s, 0, h, 0, 0))
    return pl.pallas_call(
        cross_kernel,
        grid=(shots, halves),
        in_specs=[spec, spec],
        out_specs=pl.BlockSpec((targets, 1, 1, rows, ny), lambda s, h: (0, h, s, 0, 0)),
        out_shape=jax.ShapeDtypeStruct((targets, halves, shots, rows, ny), jnp.bfloat16),
        scratch_shapes=[pltpu.VMEM(((nx + 4) * p, ny), jnp.float32)],
        compiler_params=pltpu.CompilerParams(vmem_limit_bytes=48 << 20),
        name="cross",
    )(source, receiver)


def prepare_kernel(place, group_ref, w1_ref, b1_ref, w2_ref, b2_ref, k1_ref, k2_ref, bias_ref):
    co, ci = w1_ref.shape[1:]
    shots = group_ref.shape[0] // 4
    i = place()[0]
    w = k1_ref.shape[1]
    r = lax.broadcasted_iota(jnp.int32, (ci, w), 0)
    c = lax.broadcasted_iota(jnp.int32, (ci, w), 1)
    label = jnp.full((ci, w), -1, jnp.int32)
    for k in range(4):
        for s in range(shots):
            label = jnp.where(c % SC == k * shots + s, group_ref[(i ^ k) * shots + s], label)
    hit = r == label
    acc = jnp.zeros((3 * co, w), jnp.float32)
    for t in range(9):
        pick = jnp.where(hit & (c // SC == t), 1.0, 0.0).astype(jnp.bfloat16)
        left = jnp.concatenate([w1_ref[3 * t + dy] for dy in range(3)], axis=0)
        acc = acc + jnp.dot(left, pick, preferred_element_type=jnp.float32)
        for dy in range(3):
            k2_ref[dy * co : (dy + 1) * co, t * co : (t + 1) * co] = w2_ref[3 * t + dy]
    k1_ref[...] = acc.astype(jnp.bfloat16)
    eye = lax.broadcasted_iota(jnp.int32, (co, co), 0) == lax.broadcasted_iota(jnp.int32, (co, co), 1)
    for n, b in enumerate((b1_ref, b2_ref)):
        col = jnp.sum(jnp.where(eye, jnp.broadcast_to(b[...], (co, co)), 0.0), axis=1, keepdims=True)
        bias_ref[n] = jnp.broadcast_to(col, bias_ref.shape[1:])

def prepare(place, shot_group, w1, b1, w2, b2, ny):
    co, ci = w1.shape[:2]
    w1t = w1.transpose(2, 3, 4, 0, 1).reshape(27, co, ci)
    w2t = w2.transpose(2, 3, 4, 0, 1).reshape(27, co, co)
    vmem = pl.BlockSpec(memory_space=pltpu.VMEM)
    return pl.pallas_call(
        functools.partial(prepare_kernel, place),
        in_specs=[pl.BlockSpec(memory_space=pltpu.SMEM)] + [vmem] * 4,
        out_specs=[vmem] * 3,
        out_shape=[
            jax.ShapeDtypeStruct((3 * co, 9 * SC), jnp.bfloat16),
            jax.ShapeDtypeStruct((3 * co, 9 * co), jnp.bfloat16),
            jax.ShapeDtypeStruct((2, co, ny), jnp.float32),
        ],
        name="prepare",
    )(shot_group, w1t, b1.reshape(1, co), w2t, b2.reshape(1, co))

def spread(part_ref, x, bias):
    co, ny = bias.shape
    at = slice(x * ny, (x + 1) * ny)
    lane = lax.broadcasted_iota(jnp.int32, (co, ny), 1)
    low = jnp.where(lane == 0, 0.0, pltpu.roll(part_ref[:co, at], 1, 1))
    high = jnp.where(lane == ny - 1, 0.0, pltpu.roll(part_ref[2 * co :, at], ny - 1, 1))
    return jnp.maximum(part_ref[co : 2 * co, at] + low + high + bias, 0.0)

def multiply(k_ref, v_ref, z, columns, part_ref):
    ny = v_ref.shape[-1]
    for x in range(0, columns, 2):
        right = jnp.concatenate(
            [jnp.concatenate([v_ref[z + dz, x + q + dx] for dz in range(3) for dx in range(3)], axis=0) for q in range(2)], axis=1)
        part_ref[:, x * ny : (x + 2) * ny] = jnp.dot(k_ref[...], right, preferred_element_type=jnp.float32)

def conv_kernel(place, group_ref, p0, p1, p2, p3, k1_ref, k2_ref, bias_ref,
                out_ref, x_ref, h_ref, gather_ref, a0, a1, b0, b1, t0, t1):
    ny = x_ref.shape[-1]
    nhx = h_ref.shape[1]
    co, zs, nox = out_ref.shape[:3]
    nh, shots, rows = p0.shape[:3]
    per = 2
    i, ni, j, nj = place()
    parts1, parts2, turns = (a0, a1), (b0, b1), (t0, t1)

    def lay(l):
        want = l + jnp.where(i == 0, -1, jnp.where(i == ni - 1, 1, 0))
        here = jnp.clip(want, 0, nh - 1)
        keep = jnp.where((want == here) & (l < nh), 1.0, 0.0)
        for k, p in enumerate((p0, p1, p2, p3)):
            for s in range(shots):
                gather_ref[pl.ds(k * shots + s, rows, stride=SC), :] = p[here, s].astype(jnp.float32) * keep
        for x in range(rows // per):
            for z in range(per):
                at = (x * per + z) * SC
                x_ref[l * per + z, x] = gather_ref[at : at + SC, :].astype(jnp.bfloat16)

    def hide(row, part_ref, live):
        for x in range(nhx):
            v = spread(part_ref, x, bias_ref[0])
            keep = live
            if x == 0:
                keep = live & (j > 0)
            if x == nhx - 1:
                keep = live & (j < nj - 1)
            h_ref[row, x] = jnp.where(keep, v, 0.0).astype(h_ref.dtype)

    def emit(row, part_ref, turn_ref):
        for x in range(nox):
            turn_ref[pl.ds(x, co, stride=nox), :] = spread(part_ref, x, bias_ref[1])
        out_ref[:, row] = turn_ref[...].reshape(co, nox, ny).astype(out_ref.dtype)

    gather_ref[...] = jnp.zeros(gather_ref.shape, jnp.float32)
    ahead = 5
    for l in range(ahead):
        lay(l)
    for row in range(4):
        multiply(k1_ref, x_ref, row, nhx, parts1[row % 2])
        hide(row, parts1[row % 2], (i > 0) if row == 0 else (i >= 0))
    multiply(k1_ref, x_ref, 4, nhx, a1)

    @pl.when(group_ref[0] < 0)
    def _():
        for n in range(2):
            out_ref[n, 0] = parts1[n][0:nox, 0:ny].astype(out_ref.dtype)
            out_ref[n, 1] = parts2[n][0:nox, 0:ny].astype(out_ref.dtype)
            out_ref[n, 2] = turns[n][0:nox, :].astype(out_ref.dtype)
        out_ref[2, 0] = h_ref[-group_ref[0], 0, 0:nox, :]
        out_ref[3, 0] = x_ref[-group_ref[0], 0, 0:nox, :]

    @pl.loop(0, zs // 2)
    def _(p):
        for u in range(2):
            z = 2 * p + u
            multiply(k2_ref, h_ref, z, nox, parts2[u])
            multiply(k1_ref, x_ref, z + 5, nhx, parts1[u])
            hide(z + 4, parts1[1 - u], (z + 4 != zs + 1) | (i < ni - 1))
            emit(jnp.maximum(z - 1, 0), parts2[1 - u], turns[u])
        lay(p + ahead)
    emit(zs - 1, parts2[1], t0)

def convolutions(place, shot_group, pieces, w1, b1, w2, b2):
    nh, shots, rows, ny = pieces[0].shape
    nz = nh * 2 - 4
    nx = rows // 2 - 4
    co = w1.shape[0]
    k1, k2, bias = prepare(place, shot_group, w1, b1, w2, b2, ny)
    vmem = pl.BlockSpec(memory_space=pltpu.VMEM)
    f32 = jnp.float32
    return pl.pallas_call(
        functools.partial(conv_kernel, place),
        in_specs=[pl.BlockSpec(memory_space=pltpu.SMEM)] + [vmem] * 7,
        out_specs=vmem,
        out_shape=jax.ShapeDtypeStruct((co, nz, nx, ny), jnp.bfloat16),
        scratch_shapes=[
            pltpu.VMEM((nz + 10, nx + 4, SC, ny), jnp.bfloat16),
            pltpu.VMEM((nz + 4, nx + 2, co, ny), jnp.bfloat16),
            pltpu.VMEM((rows * SC, ny), f32),
            pltpu.VMEM((3 * co, (nx + 2) * ny), f32),
            pltpu.VMEM((3 * co, (nx + 2) * ny), f32),
            pltpu.VMEM((3 * co, nx * ny), f32),
            pltpu.VMEM((3 * co, nx * ny), f32),
            pltpu.VMEM((nx * co, ny), f32),
            pltpu.VMEM((nx * co, ny), f32),
        ],
        compiler_params=pltpu.CompilerParams(vmem_limit_bytes=40 << 20),
        name="convolutions",
    )(shot_group, *pieces, k1, k2, bias)

def shards(source, receiver, shot_group, w1, b1, w2, b2):
    ni, nj = lax.axis_size("shot"), lax.axis_size("slab")
    i = lax.axis_index("shot")
    pieces = cross_pieces(source, receiver, nj)
    swapped = lax.all_to_all(pieces, "slab", 0, 0, tiled=True)
    halves = swapped.reshape((-1,) + swapped.shape[2:])
    span = halves.shape[0] // ni
    here = []
    for k in range(ni):
        start = jnp.clip((i ^ k) * span - 1, 0, halves.shape[0] - span - 2)
        part = lax.dynamic_slice_in_dim(halves, start, span + 2, 0)
        here.append(part if k == 0 else lax.ppermute(part, "shot", [(a, a ^ k) for a in range(ni)]))
    place = lambda: (lax.axis_index("shot"), ni, lax.axis_index("slab"), nj)
    return convolutions(place, shot_group, here, w1, b1, w2, b2)


def solution(mesh):
    fields = P("shot", None, "slab", None, None)
    return jax.shard_map(
        shards, mesh=mesh, in_specs=(fields, fields, P(), P(), P(), P(), P()),
        out_specs=P(None, "shot", "slab", None), check_vma=False)
```

```python
import functools

import jax
import jax.numpy as jnp
from jax import lax
from jax.experimental import pallas as pl
from jax.experimental.pallas import tpu as pltpu
from jax.sharding import PartitionSpec as P

SC = 16

def cross_kernel(src_ref, rec_ref, out_ref, wide_ref):
    planes, nx, ny = src_ref.shape[2:]
    first = (pl.program_id(0) == 0) & (pl.program_id(1) == 0)
    edge = 2 * planes
    @pl.when(first)
    def _():
        wide_ref[0:edge, :] = jnp.zeros((edge, ny), jnp.float32)
        wide_ref[edge + planes * nx :, :] = jnp.zeros((edge, ny), jnp.float32)
    for z in range(planes):
        total = jnp.zeros((nx, ny), jnp.float32)
        for t in range(src_ref.shape[1]):
            total = total + src_ref[0, t, z].astype(jnp.float32) * rec_ref[0, t, z].astype(jnp.float32)
        wide_ref[pl.ds(edge + z, nx, stride=planes), :] = total
    rows = out_ref.shape[3]
    step = rows - 2 * edge
    for d in range(out_ref.shape[0]):
        out_ref[d, 0, 0] = wide_ref[d * step : d * step + rows, :].astype(out_ref.dtype)

def cross_pieces(source, receiver, targets):
    shots, steps, planes, nx, ny = source.shape
    halves = 2
    p = planes // halves
    rows = (nx // targets + 4) * p
    spec = pl.BlockSpec((1, steps, p, nx, ny), lambda s, h: (s, 0, h, 0, 0))
    return pl.pallas_call(
        cross_kernel,
        grid=(shots, halves),
        in_specs=[spec, spec],
        out_specs=pl.BlockSpec((targets, 1, 1, rows, ny), lambda s, h: (0, h, s, 0, 0)),
        out_shape=jax.ShapeDtypeStruct((targets, halves, shots, rows, ny), jnp.bfloat16),
        scratch_shapes=[pltpu.VMEM(((nx + 4) * p, ny), jnp.float32)],
        compiler_params=pltpu.CompilerParams(vmem_limit_bytes=48 << 20),
        name="cross",
    )(source, receiver)


def prepare_kernel(place, group_ref, w1_ref, b1_ref, w2_ref, b2_ref, k1_ref, k2_ref, bias_ref):
    co, ci = w1_ref.shape[1:]
    shots = group_ref.shape[0] // 4
    i = place()[0]
    w = k1_ref.shape[1]
    r = lax.broadcasted_iota(jnp.int32, (ci, w), 0)
    c = lax.broadcasted_iota(jnp.int32, (ci, w), 1)
    label = jnp.full((ci, w), -1, jnp.int32)
    for k in range(4):
        for s in range(shots):
            label = jnp.where(c % SC == k * shots + s, group_ref[(i ^ k) * shots + s], label)
    hit = r == label
    acc = jnp.zeros((3 * co, w), jnp.float32)
    for t in range(9):
        pick = jnp.where(hit & (c // SC == t), 1.0, 0.0).astype(jnp.bfloat16)
        left = jnp.concatenate([w1_ref[3 * t + dy] for dy in range(3)], axis=0)
        acc = acc + jnp.dot(left, pick, preferred_element_type=jnp.float32)
        for dy in range(3):
            k2_ref[dy * co : (dy + 1) * co, t * co : (t + 1) * co] = w2_ref[3 * t + dy]
    k1_ref[...] = acc.astype(jnp.bfloat16)
    eye = lax.broadcasted_iota(jnp.int32, (co, co), 0) == lax.broadcasted_iota(jnp.int32, (co, co), 1)
    for n, b in enumerate((b1_ref, b2_ref)):
        col = jnp.sum(jnp.where(eye, jnp.broadcast_to(b[...], (co, co)), 0.0), axis=1, keepdims=True)
        bias_ref[n] = jnp.broadcast_to(col, bias_ref.shape[1:])

def prepare(place, shot_group, w1, b1, w2, b2, ny):
    co, ci = w1.shape[:2]
    w1t = w1.transpose(2, 3, 4, 0, 1).reshape(27, co, ci)
    w2t = w2.transpose(2, 3, 4, 0, 1).reshape(27, co, co)
    vmem = pl.BlockSpec(memory_space=pltpu.VMEM)
    return pl.pallas_call(
        functools.partial(prepare_kernel, place),
        in_specs=[pl.BlockSpec(memory_space=pltpu.SMEM)] + [vmem] * 4,
        out_specs=[vmem] * 3,
        out_shape=[
            jax.ShapeDtypeStruct((3 * co, 9 * SC), jnp.bfloat16),
            jax.ShapeDtypeStruct((3 * co, 9 * co), jnp.bfloat16),
            jax.ShapeDtypeStruct((2, co, ny), jnp.float32),
        ],
        name="prepare",
    )(shot_group, w1t, b1.reshape(1, co), w2t, b2.reshape(1, co))

def spread(part_ref, x, bias):
    co, ny = bias.shape
    at = slice(x * ny, (x + 1) * ny)
    lane = lax.broadcasted_iota(jnp.int32, (co, ny), 1)
    low = jnp.where(lane == 0, 0.0, pltpu.roll(part_ref[:co, at], 1, 1))
    high = jnp.where(lane == ny - 1, 0.0, pltpu.roll(part_ref[2 * co :, at], ny - 1, 1))
    return jnp.maximum(part_ref[co : 2 * co, at] + low + high + bias, 0.0)

def multiply(k_ref, v_ref, z, columns, part_ref):
    ny = v_ref.shape[-1]
    for x in range(0, columns, 2):
        right = jnp.concatenate(
            [jnp.concatenate([v_ref[z + dz, x + q + dx] for dz in range(3) for dx in range(3)], axis=0) for q in range(2)], axis=1)
        part_ref[:, x * ny : (x + 2) * ny] = jnp.dot(k_ref[...], right, preferred_element_type=jnp.float32)

def conv_kernel(place, first, last, group_ref, *refs):
    early = () if first else refs[:4]
    refs = refs if first else refs[4:]
    late, (k1_hbm, k2_hbm, bias_hbm), refs = refs[:4], refs[4:7], refs[7:]
    if not first:
        done_hbm, refs = refs[0], refs[1:]
    (out_hbm, k1_ref, k2_ref, bias_ref, out_ref, x_ref, h_ref, gather_ref, a0, a1, b0, b1, t0, t1, sems) = refs
    ny = x_ref.shape[-1]
    nhx = h_ref.shape[1]
    co, zs, nox = out_ref.shape[:3]
    shots, rows = late[0].shape[1:3]
    per = 2
    i, ni, j, nj = place()
    parts1, parts2, turns = (a0, a1), (b0, b1), (t0, t1)
    skip = 0 if first else per
    base = out_hbm.shape[1] - zs

    fetches = [pltpu.make_async_copy(src, dst, sems.at[n]) for n, (src, dst) in
               enumerate(((k1_hbm, k1_ref), (k2_hbm, k2_ref), (bias_hbm, bias_ref)))]
    for f in fetches:
        f.start()
    if not first:
        carry = pltpu.make_async_copy(done_hbm, out_hbm.at[:, :base], sems.at[3])
        carry.start()

    def lay(l):
        if isinstance(l, int) and l < skip:
            source, nh = early, early[0].shape[0]
            want = l + nh - skip - jnp.where(i == 0, 1, 0)
        else:
            source, nh = late, late[0].shape[0]
            want = l - skip
            if first:
                want = want - jnp.where(i == 0, 1, 0)
            if last:
                want = want + jnp.where(i == ni - 1, 1, 0)
        here = jnp.clip(want, 0, nh - 1)
        keep = jnp.where(want == here, 1.0, 0.0)
        for k, p in enumerate(source):
            for s in range(shots):
                gather_ref[pl.ds(k * shots + s, rows, stride=SC), :] = p[here, s].astype(jnp.float32) * keep
        for x in range(rows // per):
            for z in range(per):
                at = (x * per + z) * SC
                x_ref[l * per + z, x] = gather_ref[at : at + SC, :].astype(jnp.bfloat16)

    def hide(row, part_ref, live):
        for x in range(nhx):
            v = spread(part_ref, x, bias_ref[0])
            keep = live
            if x == 0:
                keep = live & (j > 0)
            if x == nhx - 1:
                keep = live & (j < nj - 1)
            h_ref[row, x] = jnp.where(keep, v, 0.0).astype(h_ref.dtype)

    def emit(row, part_ref, turn_ref):
        for x in range(nox):
            turn_ref[pl.ds(x, co, stride=nox), :] = spread(part_ref, x, bias_ref[1])
        out_ref[:, row] = turn_ref[...].reshape(co, nox, ny).astype(out_ref.dtype)

    gather_ref[...] = jnp.zeros(gather_ref.shape, jnp.float32)
    ahead = 5
    for l in range(ahead):
        lay(l)
    for f in fetches:
        f.wait()
    for row in range(4):
        multiply(k1_ref, x_ref, row, nhx, parts1[row % 2])
        hide(row, parts1[row % 2], (i > 0) if first and row == 0 else (i >= 0))
    multiply(k1_ref, x_ref, 4, nhx, a1)

    @pl.when(group_ref[0] < 0)
    def _():
        for n in range(2):
            out_ref[n, 0] = parts1[n][0:nox, 0:ny].astype(out_ref.dtype)
            out_ref[n, 1] = parts2[n][0:nox, 0:ny].astype(out_ref.dtype)
            out_ref[n, 2] = turns[n][0:nox, :].astype(out_ref.dtype)
        out_ref[2, 0] = h_ref[-group_ref[0], 0, 0:nox, :]
        out_ref[3, 0] = x_ref[-group_ref[0], 0, 0:nox, :]

    def pair(p):
        for u in range(2):
            z = 2 * p + u
            multiply(k2_ref, h_ref, z, nox, parts2[u])
            multiply(k1_ref, x_ref, z + 5, nhx, parts1[u])
            hide(z + 4, parts1[1 - u], ((z + 4 != zs + 1) | (i < ni - 1)) if last else (i >= 0))
            emit(jnp.maximum(z - 1, 0), parts2[1 - u], turns[u])
        lay(p + ahead)

    pairs = zs // 2
    cut = pairs - 3
    ready = 2 * cut - 1
    pl.loop(0, cut)(pair)
    head = pltpu.make_async_copy(out_ref.at[:, :ready], out_hbm.at[:, base : base + ready], sems.at[4])
    head.start()
    pl.loop(cut, pairs)(pair)
    emit(zs - 1, parts2[1], t0)
    tail = pltpu.make_async_copy(out_ref.at[:, ready:], out_hbm.at[:, base + ready :], sems.at[5])
    tail.start()
    head.wait()
    tail.wait()
    if not first:
        carry.wait()


def convolutions(place, shot_group, early, late, done, weights, out_rows, last):
    first = early is None
    shots, rows, ny = late[0].shape[1:]
    halves = late[0].shape[0] + (0 if first else 2)
    nz = halves * 2 - 4
    nx = rows // 2 - 4
    k1, k2, bias = weights
    co = bias.shape[1]
    vmem = pl.BlockSpec(memory_space=pltpu.VMEM)
    hbm = pl.BlockSpec(memory_space=pl.ANY)
    f32 = jnp.float32
    pieces = list(late) if first else list(early) + list(late)
    more = [] if first else [done]
    return pl.pallas_call(
        functools.partial(conv_kernel, place, first, last),
        in_specs=[pl.BlockSpec(memory_space=pltpu.SMEM)] + [vmem] * len(pieces) + [hbm] * (3 + len(more)),
        out_specs=hbm,
        out_shape=jax.ShapeDtypeStruct((co, out_rows, nx, ny), jnp.bfloat16),
        scratch_shapes=[
            pltpu.VMEM(k1.shape, k1.dtype),
            pltpu.VMEM(k2.shape, k2.dtype),
            pltpu.VMEM(bias.shape, bias.dtype),
            pltpu.VMEM((co, nz, nx, ny), jnp.bfloat16),
            pltpu.VMEM((nz + 10, nx + 4, SC, ny), jnp.bfloat16),
            pltpu.VMEM((nz + 4, nx + 2, co, ny), jnp.bfloat16),
            pltpu.VMEM((rows * SC, ny), f32),
            pltpu.VMEM((3 * co, (nx + 2) * ny), f32),
            pltpu.VMEM((3 * co, (nx + 2) * ny), f32),
            pltpu.VMEM((3 * co, nx * ny), f32),
            pltpu.VMEM((3 * co, nx * ny), f32),
            pltpu.VMEM((nx * co, ny), f32),
            pltpu.VMEM((nx * co, ny), f32),
            pltpu.SemaphoreType.DMA((6,)),
        ],
        compiler_params=pltpu.CompilerParams(vmem_limit_bytes=20 << 20),
        name="head" if first else "tail",
    )(shot_group, *pieces, k1, k2, bias, *more)


def shards(source, receiver, shot_group, w1, b1, w2, b2):
    ni, nj = lax.axis_size("shot"), lax.axis_size("slab")
    i = lax.axis_index("shot")
    place = lambda: (lax.axis_index("shot"), ni, lax.axis_index("slab"), nj)
    weights = prepare(place, shot_group, w1, b1, w2, b2, source.shape[-1])
    pieces = cross_pieces(source, receiver, nj)
    swapped = lax.all_to_all(pieces, "slab", 0, 0, tiled=True)
    halves = swapped.reshape((-1,) + swapped.shape[2:])
    span = halves.shape[0] // ni
    chunks = []
    for low, size in ((-1, span // 2 + 2), (span // 2 + 1, span // 2)):
        here = []
        for k in range(ni):
            start = jnp.clip((i ^ k) * span + low, 0, halves.shape[0] - size)
            part = lax.dynamic_slice_in_dim(halves, start, size, 0)
            here.append(part if k == 0 else lax.ppermute(part, "shot", [(a, a ^ k) for a in range(ni)]))
        chunks.append(here)
    rows = source.shape[2] * nj // ni
    top = convolutions(place, shot_group, None, chunks[0], None, weights, rows // 2, False)
    return convolutions(place, shot_group, chunks[0], chunks[1], top, weights, rows, True)


def solution(mesh):
    fields = P("shot", None, "slab", None, None)
    return jax.shard_map(
        shards, mesh=mesh, in_specs=(fields, fields, P(), P(), P(), P(), P()),
        out_specs=P(None, "shot", "slab", None), check_vma=False)
```

```python
import functools

import jax
import jax.numpy as jnp
from jax import lax
from jax.experimental import pallas as pl
from jax.experimental.pallas import tpu as pltpu
from jax.sharding import PartitionSpec as P

SC = 16

def cross_kernel(src_ref, rec_ref, out_ref, wide_ref):
    planes, nx, ny = src_ref.shape[2:]
    first = (pl.program_id(0) == 0) & (pl.program_id(1) == 0)
    edge = 2 * planes
    @pl.when(first)
    def _():
        wide_ref[0:edge, :] = jnp.zeros((edge, ny), jnp.float32)
        wide_ref[edge + planes * nx :, :] = jnp.zeros((edge, ny), jnp.float32)
    strip = 32
    for z in range(planes):
        for x in range(0, nx, strip):
            total = None
            for t in range(src_ref.shape[1]):
                term = src_ref[0, t, z, x : x + strip].astype(jnp.float32) * rec_ref[0, t, z, x : x + strip].astype(jnp.float32)
                total = term if total is None else total + term
            wide_ref[pl.ds(edge + z + x * planes, strip, stride=planes), :] = total
    rows = out_ref.shape[3]
    step = rows - 2 * edge
    for d in range(out_ref.shape[0]):
        out_ref[d, 0, 0] = wide_ref[d * step : d * step + rows, :].astype(out_ref.dtype)

def cross_pieces(source, receiver, targets):
    shots, steps, planes, nx, ny = source.shape
    halves = 2
    p = planes // halves
    rows = (nx // targets + 4) * p
    spec = pl.BlockSpec((1, steps, p, nx, ny), lambda s, h: (s, 0, h, 0, 0))
    return pl.pallas_call(
        cross_kernel,
        grid=(shots, halves),
        in_specs=[spec, spec],
        out_specs=pl.BlockSpec((targets, 1, 1, rows, ny), lambda s, h: (0, h, s, 0, 0)),
        out_shape=jax.ShapeDtypeStruct((targets, halves, shots, rows, ny), jnp.bfloat16),
        scratch_shapes=[pltpu.VMEM(((nx + 4) * p, ny), jnp.float32)],
        compiler_params=pltpu.CompilerParams(vmem_limit_bytes=48 << 20),
        name="cross",
    )(source, receiver)


def prepare_kernel(place, group_ref, w1_ref, b1_ref, w2_ref, b2_ref, k1_ref, k2_ref, bias_ref):
    co, ci = w1_ref.shape[1:]
    shots = group_ref.shape[0] // 4
    i = place()[0]
    w = k1_ref.shape[1]
    r = lax.broadcasted_iota(jnp.int32, (ci, w), 0)
    c = lax.broadcasted_iota(jnp.int32, (ci, w), 1)
    label = jnp.full((ci, w), -1, jnp.int32)
    for k in range(4):
        for s in range(shots):
            label = jnp.where(c % SC == k * shots + s, group_ref[(i ^ k) * shots + s], label)
    hit = r == label
    acc = jnp.zeros((3 * co, w), jnp.float32)
    for t in range(9):
        pick = jnp.where(hit & (c // SC == t), 1.0, 0.0).astype(jnp.bfloat16)
        left = jnp.concatenate([w1_ref[3 * t + dy] for dy in range(3)], axis=0)
        acc = acc + jnp.dot(left, pick, preferred_element_type=jnp.float32)
        for dy in range(3):
            k2_ref[dy * co : (dy + 1) * co, t * co : (t + 1) * co] = w2_ref[3 * t + dy]
    k1_ref[...] = acc.astype(jnp.bfloat16)
    eye = lax.broadcasted_iota(jnp.int32, (co, co), 0) == lax.broadcasted_iota(jnp.int32, (co, co), 1)
    for n, b in enumerate((b1_ref, b2_ref)):
        col = jnp.sum(jnp.where(eye, jnp.broadcast_to(b[...], (co, co)), 0.0), axis=1, keepdims=True)
        bias_ref[n] = jnp.broadcast_to(col, bias_ref.shape[1:])

def prepare(place, shot_group, w1, b1, w2, b2, ny):
    co, ci = w1.shape[:2]
    w1t = w1.transpose(2, 3, 4, 0, 1).reshape(27, co, ci)
    w2t = w2.transpose(2, 3, 4, 0, 1).reshape(27, co, co)
    vmem = pl.BlockSpec(memory_space=pltpu.VMEM)
    return pl.pallas_call(
        functools.partial(prepare_kernel, place),
        in_specs=[pl.BlockSpec(memory_space=pltpu.SMEM)] + [vmem] * 4,
        out_specs=[vmem] * 3,
        out_shape=[
            jax.ShapeDtypeStruct((3 * co, 9 * SC), jnp.bfloat16),
            jax.ShapeDtypeStruct((3 * co, 9 * co), jnp.bfloat16),
            jax.ShapeDtypeStruct((2, co, ny), jnp.float32),
        ],
        name="prepare",
    )(shot_group, w1t, b1.reshape(1, co), w2t, b2.reshape(1, co))

def spread(part_ref, x, bias):
    co, ny = bias.shape
    at = slice(x * ny, (x + 1) * ny)
    lane = lax.broadcasted_iota(jnp.int32, (co, ny), 1)
    low = jnp.where(lane == 0, 0.0, pltpu.roll(part_ref[:co, at], 1, 1))
    high = jnp.where(lane == ny - 1, 0.0, pltpu.roll(part_ref[2 * co :, at], ny - 1, 1))
    return jnp.maximum(part_ref[co : 2 * co, at] + low + high + bias, 0.0)

def multiply(k_ref, v_ref, z, columns, part_ref):
    ny = v_ref.shape[-1]
    for x in range(0, columns, 2):
        right = jnp.concatenate(
            [jnp.concatenate([v_ref[z + dz, x + q + dx] for dz in range(3) for dx in range(3)], axis=0) for q in range(2)], axis=1)
        part_ref[:, x * ny : (x + 2) * ny] = jnp.dot(k_ref[...], right, preferred_element_type=jnp.float32)

def conv_kernel(place, first, last, group_ref, *refs):
    early = () if first else refs[:4]
    refs = refs if first else refs[4:]
    late, (k1_hbm, k2_hbm, bias_hbm), refs = refs[:4], refs[4:7], refs[7:]
    if not first:
        done_hbm, refs = refs[0], refs[1:]
    (out_hbm, k1_ref, k2_ref, bias_ref, out_ref, x_ref, h_ref, gather_ref, a0, a1, b0, b1, t0, t1, sems) = refs
    ny = x_ref.shape[-1]
    nhx = h_ref.shape[1]
    co, zs, nox = out_ref.shape[:3]
    shots, rows = late[0].shape[1:3]
    per = 2
    i, ni, j, nj = place()
    parts1, parts2, turns = (a0, a1), (b0, b1), (t0, t1)
    skip = 0 if first else per
    base = out_hbm.shape[1] - zs

    fetches = [pltpu.make_async_copy(src, dst, sems.at[n]) for n, (src, dst) in
               enumerate(((k1_hbm, k1_ref), (k2_hbm, k2_ref), (bias_hbm, bias_ref)))]
    for f in fetches:
        f.start()
    if not first:
        carry = pltpu.make_async_copy(done_hbm, out_hbm.at[:, :base], sems.at[3])
        carry.start()

    def lay(l):
        if isinstance(l, int) and l < skip:
            source, nh = early, early[0].shape[0]
            want = l + nh - skip - jnp.where(i == 0, 1, 0)
        else:
            source, nh = late, late[0].shape[0]
            want = l - skip
            if first:
                want = want - jnp.where(i == 0, 1, 0)
            if last:
                want = want + jnp.where(i == ni - 1, 1, 0)
        here = jnp.clip(want, 0, nh - 1)
        keep = jnp.where(want == here, 1.0, 0.0)
        for k, p in enumerate(source):
            for s in range(shots):
                gather_ref[pl.ds(k * shots + s, rows, stride=SC), :] = p[here, s].astype(jnp.float32) * keep
        for x in range(rows // per):
            for z in range(per):
                at = (x * per + z) * SC
                x_ref[l * per + z, x] = gather_ref[at : at + SC, :].astype(jnp.bfloat16)

    def hide(row, part_ref, live):
        for x in range(nhx):
            v = spread(part_ref, x, bias_ref[0])
            keep = live
            if x == 0:
                keep = live & (j > 0)
            if x == nhx - 1:
                keep = live & (j < nj - 1)
            h_ref[row, x] = jnp.where(keep, v, 0.0).astype(h_ref.dtype)

    def emit(row, part_ref, turn_ref):
        for x in range(nox):
            turn_ref[pl.ds(x, co, stride=nox), :] = spread(part_ref, x, bias_ref[1])
        out_ref[:, row] = turn_ref[...].reshape(co, nox, ny).astype(out_ref.dtype)

    gather_ref[...] = jnp.zeros(gather_ref.shape, jnp.float32)
    ahead = 5
    for l in range(ahead):
        lay(l)
    for f in fetches:
        f.wait()
    for row in range(4):
        multiply(k1_ref, x_ref, row, nhx, parts1[row % 2])
        hide(row, parts1[row % 2], (i > 0) if first and row == 0 else (i >= 0))
    multiply(k1_ref, x_ref, 4, nhx, a1)

    @pl.when(group_ref[0] < 0)
    def _():
        for n in range(2):
            out_ref[n, 0] = parts1[n][0:nox, 0:ny].astype(out_ref.dtype)
            out_ref[n, 1] = parts2[n][0:nox, 0:ny].astype(out_ref.dtype)
            out_ref[n, 2] = turns[n][0:nox, :].astype(out_ref.dtype)
        out_ref[2, 0] = h_ref[-group_ref[0], 0, 0:nox, :]
        out_ref[3, 0] = x_ref[-group_ref[0], 0, 0:nox, :]

    def pair(p):
        for u in range(2):
            z = 2 * p + u
            multiply(k2_ref, h_ref, z, nox, parts2[u])
            multiply(k1_ref, x_ref, z + 5, nhx, parts1[u])
            hide(z + 4, parts1[1 - u], ((z + 4 != zs + 1) | (i < ni - 1)) if last else (i >= 0))
            emit(jnp.maximum(z - 1, 0), parts2[1 - u], turns[u])
        lay(p + ahead)

    pairs = zs // 2
    cut = pairs - 3
    ready = 2 * cut - 1
    pl.loop(0, cut)(pair)
    head = pltpu.make_async_copy(out_ref.at[:, :ready], out_hbm.at[:, base : base + ready], sems.at[4])
    head.start()
    pl.loop(cut, pairs)(pair)
    emit(zs - 1, parts2[1], t0)
    tail = pltpu.make_async_copy(out_ref.at[:, ready:], out_hbm.at[:, base + ready :], sems.at[5])
    tail.start()
    head.wait()
    tail.wait()
    if not first:
        carry.wait()


def convolutions(place, shot_group, early, late, done, weights, out_rows, last):
    first = early is None
    shots, rows, ny = late[0].shape[1:]
    halves = late[0].shape[0] + (0 if first else 2)
    nz = halves * 2 - 4
    nx = rows // 2 - 4
    k1, k2, bias = weights
    co = bias.shape[1]
    vmem = pl.BlockSpec(memory_space=pltpu.VMEM)
    hbm = pl.BlockSpec(memory_space=pl.ANY)
    f32 = jnp.float32
    pieces = list(late) if first else list(early) + list(late)
    more = [] if first else [done]
    return pl.pallas_call(
        functools.partial(conv_kernel, place, first, last),
        in_specs=[pl.BlockSpec(memory_space=pltpu.SMEM)] + [vmem] * len(pieces) + [pl.BlockSpec(memory_space=pltpu.HBM)] * 3 + [hbm] * len(more),
        out_specs=hbm,
        out_shape=jax.ShapeDtypeStruct((co, out_rows, nx, ny), jnp.bfloat16),
        scratch_shapes=[
            pltpu.VMEM(k1.shape, k1.dtype),
            pltpu.VMEM(k2.shape, k2.dtype),
            pltpu.VMEM(bias.shape, bias.dtype),
            pltpu.VMEM((co, nz, nx, ny), jnp.bfloat16),
            pltpu.VMEM((nz + 10, nx + 4, SC, ny), jnp.bfloat16),
            pltpu.VMEM((nz + 4, nx + 2, co, ny), jnp.bfloat16),
            pltpu.VMEM((rows * SC, ny), f32),
            pltpu.VMEM((3 * co, (nx + 2) * ny), f32),
            pltpu.VMEM((3 * co, (nx + 2) * ny), f32),
            pltpu.VMEM((3 * co, nx * ny), f32),
            pltpu.VMEM((3 * co, nx * ny), f32),
            pltpu.VMEM((nx * co, ny), f32),
            pltpu.VMEM((nx * co, ny), f32),
            pltpu.SemaphoreType.DMA((6,)),
        ],
        compiler_params=pltpu.CompilerParams(vmem_limit_bytes=20 << 20),
        name="head" if first else "tail",
    )(shot_group, *pieces, k1, k2, bias, *more)


def shards(source, receiver, shot_group, w1, b1, w2, b2):
    ni, nj = lax.axis_size("shot"), lax.axis_size("slab")
    i = lax.axis_index("shot")
    place = lambda: (lax.axis_index("shot"), ni, lax.axis_index("slab"), nj)
    weights = prepare(place, shot_group, w1, b1, w2, b2, source.shape[-1])
    pieces = cross_pieces(source, receiver, nj)
    swapped = lax.all_to_all(pieces, "slab", 0, 0, tiled=True)
    halves = swapped.reshape((-1,) + swapped.shape[2:])
    span = halves.shape[0] // ni
    chunks = []
    for low, size in ((-1, span // 2 + 2), (span // 2 + 1, span // 2)):
        here = []
        for k in range(ni):
            start = jnp.clip((i ^ k) * span + low, 0, halves.shape[0] - size)
            part = lax.dynamic_slice_in_dim(halves, start, size, 0)
            here.append(part if k == 0 else lax.ppermute(part, "shot", [(a, a ^ k) for a in range(ni)]))
        chunks.append(here)
    rows = source.shape[2] * nj // ni
    top = convolutions(place, shot_group, None, chunks[0], None, weights, rows // 2, False)
    return convolutions(place, shot_group, chunks[0], chunks[1], top, weights, rows, True)


def solution(mesh):
    fields = P("shot", None, "slab", None, None)
    return jax.shard_map(
        shards, mesh=mesh, in_specs=(fields, fields, P(), P(), P(), P(), P()),
        out_specs=P(None, "shot", "slab", None), check_vma=False)
```

```python
import functools

import jax
import jax.numpy as jnp
from jax import lax
from jax.experimental import pallas as pl
from jax.experimental.pallas import tpu as pltpu
from jax.sharding import PartitionSpec as P

SC = 16

def cross_kernel(src_ref, rec_ref, out_ref, wide_ref):
    planes, nx, ny = src_ref.shape[2:]
    first = (pl.program_id(0) == 0) & (pl.program_id(1) == 0)
    edge = 2 * planes
    @pl.when(first)
    def _():
        wide_ref[0:edge, :] = jnp.zeros((edge, ny), jnp.float32)
        wide_ref[edge + planes * nx :, :] = jnp.zeros((edge, ny), jnp.float32)
    strip = 32
    for z in range(planes):
        for x in range(0, nx, strip):
            total = None
            for t in range(src_ref.shape[1]):
                term = src_ref[0, t, z, x : x + strip].astype(jnp.float32) * rec_ref[0, t, z, x : x + strip].astype(jnp.float32)
                total = term if total is None else total + term
            wide_ref[pl.ds(edge + z + x * planes, strip, stride=planes), :] = total
    rows = out_ref.shape[3]
    step = rows - 2 * edge
    for d in range(out_ref.shape[0]):
        out_ref[d, 0, 0] = wide_ref[d * step : d * step + rows, :].astype(out_ref.dtype)

def cross_pieces(source, receiver, targets):
    shots, steps, planes, nx, ny = source.shape
    halves = 2
    p = planes // halves
    rows = (nx // targets + 4) * p
    spec = pl.BlockSpec((1, steps, p, nx, ny), lambda s, h: (s, 0, h, 0, 0))
    return pl.pallas_call(
        cross_kernel,
        grid=(shots, halves),
        in_specs=[spec, spec],
        out_specs=pl.BlockSpec((targets, 1, 1, rows, ny), lambda s, h: (0, h, s, 0, 0)),
        out_shape=jax.ShapeDtypeStruct((targets, halves, shots, rows, ny), jnp.bfloat16),
        scratch_shapes=[pltpu.VMEM(((nx + 4) * p, ny), jnp.float32)],
        compiler_params=pltpu.CompilerParams(vmem_limit_bytes=48 << 20),
        name="cross",
    )(source, receiver)


def prepare_kernel(place, group_ref, w1_ref, b1_ref, w2_ref, b2_ref, k1_ref, k2_ref, bias_ref):
    co, ci = w1_ref.shape[1:]
    shots = group_ref.shape[0] // 4
    i = place()[0]
    w = k1_ref.shape[1]
    r = lax.broadcasted_iota(jnp.int32, (ci, w), 0)
    c = lax.broadcasted_iota(jnp.int32, (ci, w), 1)
    label = jnp.full((ci, w), -1, jnp.int32)
    for k in range(4):
        for s in range(shots):
            label = jnp.where(c % SC == k * shots + s, group_ref[(i ^ k) * shots + s], label)
    hit = r == label
    k2_ref[...] = jnp.zeros(k2_ref.shape, k2_ref.dtype)
    for oz in range(2):
        acc = jnp.zeros((3 * co, w), jnp.float32)
        for t in range(9):
            column = 3 * oz + t
            pick = jnp.where(hit & (c // SC == column), 1.0, 0.0).astype(jnp.bfloat16)
            left = jnp.concatenate([w1_ref[3 * t + dy] for dy in range(3)], axis=0)
            acc = acc + jnp.dot(left, pick, preferred_element_type=jnp.float32)
            for dy in range(3):
                row = (3 * oz + dy) * co
                k2_ref[row : row + co, column * co : (column + 1) * co] = w2_ref[3 * t + dy]
        k1_ref[3 * oz * co : 3 * (oz + 1) * co, :] = acc.astype(jnp.bfloat16)
    eye = lax.broadcasted_iota(jnp.int32, (co, co), 0) == lax.broadcasted_iota(jnp.int32, (co, co), 1)
    for n, b in enumerate((b1_ref, b2_ref)):
        col = jnp.sum(jnp.where(eye, jnp.broadcast_to(b[...], (co, co)), 0.0), axis=1, keepdims=True)
        bias_ref[n] = jnp.broadcast_to(col, bias_ref.shape[1:])

def prepare(place, shot_group, w1, b1, w2, b2, ny):
    co, ci = w1.shape[:2]
    w1t = w1.transpose(2, 3, 4, 0, 1).reshape(27, co, ci)
    w2t = w2.transpose(2, 3, 4, 0, 1).reshape(27, co, co)
    vmem = pl.BlockSpec(memory_space=pltpu.VMEM)
    return pl.pallas_call(
        functools.partial(prepare_kernel, place),
        in_specs=[pl.BlockSpec(memory_space=pltpu.SMEM)] + [vmem] * 4,
        out_specs=[vmem] * 3,
        out_shape=[
            jax.ShapeDtypeStruct((6 * co, 12 * SC), jnp.bfloat16),
            jax.ShapeDtypeStruct((6 * co, 12 * co), jnp.bfloat16),
            jax.ShapeDtypeStruct((2, co, ny), jnp.float32),
        ],
        name="prepare",
    )(shot_group, w1t, b1.reshape(1, co), w2t, b2.reshape(1, co))

def spread(part_ref, oz, x, bias):
    co, ny = bias.shape
    at = slice(x * ny, (x + 1) * ny)
    low_at, mid_at, high_at = (slice((3 * oz + n) * co, (3 * oz + n + 1) * co) for n in range(3))
    lane = lax.broadcasted_iota(jnp.int32, (co, ny), 1)
    low = jnp.where(lane == 0, 0.0, pltpu.roll(part_ref[low_at, at], 1, 1))
    high = jnp.where(lane == ny - 1, 0.0, pltpu.roll(part_ref[high_at, at], ny - 1, 1))
    return jnp.maximum(part_ref[mid_at, at] + low + high + bias, 0.0)

def multiply(k_ref, v_ref, z, columns, part_ref):
    ny = v_ref.shape[-1]
    for x in range(0, columns, 2):
        right = jnp.concatenate(
            [jnp.concatenate([v_ref[z + dz, x + q + dx] for dz in range(4) for dx in range(3)], axis=0) for q in range(2)], axis=1)
        part_ref[:, x * ny : (x + 2) * ny] = jnp.dot(k_ref[...], right, preferred_element_type=jnp.float32)

def conv_kernel(place, first, last, group_ref, *refs):
    early = () if first else refs[:4]
    refs = refs if first else refs[4:]
    late, (k1_hbm, k2_hbm, bias_hbm), refs = refs[:4], refs[4:7], refs[7:]
    if not first:
        done_hbm, refs = refs[0], refs[1:]
    (out_hbm, k1_ref, k2_ref, bias_ref, out_ref, x_ref, h_ref, gather_ref, a0, a1, b0, b1, t0, t1, sems) = refs
    ny = x_ref.shape[-1]
    nhx = h_ref.shape[1]
    co, zs, nox = out_ref.shape[:3]
    shots, rows = late[0].shape[1:3]
    per = 2
    i, ni, j, nj = place()
    parts1, parts2, turns = (a0, a1), (b0, b1), (t0, t1)
    skip = 0 if first else per
    base = out_hbm.shape[1] - zs

    fetches = [pltpu.make_async_copy(src, dst, sems.at[n]) for n, (src, dst) in
               enumerate(((k1_hbm, k1_ref), (k2_hbm, k2_ref), (bias_hbm, bias_ref)))]
    for f in fetches:
        f.start()
    if not first:
        carry = pltpu.make_async_copy(done_hbm, out_hbm.at[:, :base], sems.at[3])
        carry.start()

    def lay(l):
        if isinstance(l, int) and l < skip:
            source, nh = early, early[0].shape[0]
            want = l + nh - skip - jnp.where(i == 0, 1, 0)
        else:
            source, nh = late, late[0].shape[0]
            want = l - skip
            if first:
                want = want - jnp.where(i == 0, 1, 0)
            if last:
                want = want + jnp.where(i == ni - 1, 1, 0)
        here = jnp.clip(want, 0, nh - 1)
        keep = jnp.where(want == here, 1.0, 0.0)
        for k, p in enumerate(source):
            for s in range(shots):
                gather_ref[pl.ds(k * shots + s, rows, stride=SC), :] = p[here, s].astype(jnp.float32) * keep
        for x in range(rows // per):
            for z in range(per):
                at = (x * per + z) * SC
                x_ref[l * per + z, x] = gather_ref[at : at + SC, :].astype(jnp.bfloat16)

    def hide(pair, part_ref, lives):
        for oz in range(2):
            for x in range(nhx):
                v = spread(part_ref, oz, x, bias_ref[0])
                keep = lives[oz]
                if x == 0:
                    keep = keep & (j > 0)
                if x == nhx - 1:
                    keep = keep & (j < nj - 1)
                h_ref[2 * pair + oz, x] = jnp.where(keep, v, 0.0).astype(h_ref.dtype)

    def emit(pair, part_ref):
        for oz in range(2):
            turn_ref = turns[oz]
            for x in range(nox):
                turn_ref[pl.ds(x, co, stride=nox), :] = spread(part_ref, oz, x, bias_ref[1])
            out_ref[:, 2 * pair + oz] = turn_ref[...].reshape(co, nox, ny).astype(out_ref.dtype)

    gather_ref[...] = jnp.zeros(gather_ref.shape, jnp.float32)
    ahead = 5
    for l in range(ahead):
        lay(l)
    for f in fetches:
        f.wait()
    always = i >= 0
    for pair in range(2):
        multiply(k1_ref, x_ref, 2 * pair, nhx, parts1[pair])
        hide(pair, parts1[pair], ((i > 0) if first and pair == 0 else always, always))
    multiply(k1_ref, x_ref, 4, nhx, a1)

    @pl.when(group_ref[0] < 0)
    def _():
        for n in range(2):
            out_ref[n, 0] = parts1[n][0:nox, 0:ny].astype(out_ref.dtype)
            out_ref[n, 1] = parts2[n][0:nox, 0:ny].astype(out_ref.dtype)
            out_ref[n, 2] = turns[n][0:nox, :].astype(out_ref.dtype)
        out_ref[2, 0] = h_ref[-group_ref[0], 0, 0:nox, :]
        out_ref[3, 0] = x_ref[-group_ref[0], 0, 0:nox, :]

    def quad(n):
        for u in range(2):
            p = 2 * n + u
            multiply(k2_ref, h_ref, 2 * p, nox, parts2[u])
            multiply(k1_ref, x_ref, 2 * p + 6, nhx, parts1[u])
            hide(p + 2, parts1[1 - u], (always, ((2 * p + 5 != zs + 1) | (i < ni - 1)) if last else always))
            emit(jnp.maximum(p - 1, 0), parts2[1 - u])
            lay(p + ahead)

    quads = zs // 4
    cut = quads - 1
    ready = 2 * (2 * cut - 1)
    pl.loop(0, cut)(quad)
    head = pltpu.make_async_copy(out_ref.at[:, :ready], out_hbm.at[:, base : base + ready], sems.at[4])
    head.start()
    pl.loop(cut, quads)(quad)
    emit(zs // 2 - 1, parts2[1])
    tail = pltpu.make_async_copy(out_ref.at[:, ready:], out_hbm.at[:, base + ready :], sems.at[5])
    tail.start()
    head.wait()
    tail.wait()
    if not first:
        carry.wait()


def convolutions(place, shot_group, early, late, done, weights, out_rows, last):
    first = early is None
    shots, rows, ny = late[0].shape[1:]
    halves = late[0].shape[0] + (0 if first else 2)
    nz = halves * 2 - 4
    nx = rows // 2 - 4
    k1, k2, bias = weights
    co = bias.shape[1]
    vmem = pl.BlockSpec(memory_space=pltpu.VMEM)
    hbm = pl.BlockSpec(memory_space=pl.ANY)
    f32 = jnp.float32
    pieces = list(late) if first else list(early) + list(late)
    more = [] if first else [done]
    return pl.pallas_call(
        functools.partial(conv_kernel, place, first, last),
        in_specs=[pl.BlockSpec(memory_space=pltpu.SMEM)] + [vmem] * len(pieces) + [pl.BlockSpec(memory_space=pltpu.HBM)] * 3 + [hbm] * len(more),
        out_specs=hbm,
        out_shape=jax.ShapeDtypeStruct((co, out_rows, nx, ny), jnp.bfloat16),
        scratch_shapes=[
            pltpu.VMEM(k1.shape, k1.dtype),
            pltpu.VMEM(k2.shape, k2.dtype),
            pltpu.VMEM(bias.shape, bias.dtype),
            pltpu.VMEM((co, nz, nx, ny), jnp.bfloat16),
            pltpu.VMEM((nz + 10, nx + 4, SC, ny), jnp.bfloat16),
            pltpu.VMEM((nz + 4, nx + 2, co, ny), jnp.bfloat16),
            pltpu.VMEM((rows * SC, ny), f32),
            pltpu.VMEM((6 * co, (nx + 2) * ny), f32),
            pltpu.VMEM((6 * co, (nx + 2) * ny), f32),
            pltpu.VMEM((6 * co, nx * ny), f32),
            pltpu.VMEM((6 * co, nx * ny), f32),
            pltpu.VMEM((nx * co, ny), f32),
            pltpu.VMEM((nx * co, ny), f32),
            pltpu.SemaphoreType.DMA((6,)),
        ],
        compiler_params=pltpu.CompilerParams(vmem_limit_bytes=20 << 20),
        name="head" if first else "tail",
    )(shot_group, *pieces, k1, k2, bias, *more)


def shards(source, receiver, shot_group, w1, b1, w2, b2):
    ni, nj = lax.axis_size("shot"), lax.axis_size("slab")
    i = lax.axis_index("shot")
    place = lambda: (lax.axis_index("shot"), ni, lax.axis_index("slab"), nj)
    weights = prepare(place, shot_group, w1, b1, w2, b2, source.shape[-1])
    pieces = cross_pieces(source, receiver, nj)
    swapped = lax.all_to_all(pieces, "slab", 0, 0, tiled=True)
    swapped, weights = lax.optimization_barrier((swapped, weights))
    halves = swapped.reshape((-1,) + swapped.shape[2:])
    span = halves.shape[0] // ni
    chunks = []
    for low, size in ((-1, span // 2 + 2), (span // 2 + 1, span // 2)):
        here = []
        for k in range(ni):
            start = jnp.clip((i ^ k) * span + low, 0, halves.shape[0] - size)
            part = lax.dynamic_slice_in_dim(halves, start, size, 0)
            here.append(part if k == 0 else lax.ppermute(part, "shot", [(a, a ^ k) for a in range(ni)]))
        chunks.append(here)
    rows = source.shape[2] * nj // ni
    top = convolutions(place, shot_group, None, chunks[0], None, weights, rows // 2, False)
    return convolutions(place, shot_group, chunks[0], chunks[1], top, weights, rows, True)


def solution(mesh):
    fields = P("shot", None, "slab", None, None)
    return jax.shard_map(
        shards, mesh=mesh, in_specs=(fields, fields, P(), P(), P(), P(), P()),
        out_specs=P(None, "shot", "slab", None), check_vma=False)
```

```python
import functools

import jax
import jax.numpy as jnp
from jax import lax
from jax.experimental import pallas as pl
from jax.experimental.pallas import tpu as pltpu
from jax.sharding import PartitionSpec as P

SC = 16

def cross_kernel(src_ref, rec_ref, out_ref, wide_ref):
    planes, nx, ny = src_ref.shape[2:]
    first = (pl.program_id(0) == 0) & (pl.program_id(1) == 0)
    edge = 2 * planes
    @pl.when(first)
    def _():
        wide_ref[0:edge, :] = jnp.zeros((edge, ny), jnp.float32)
        wide_ref[edge + planes * nx :, :] = jnp.zeros((edge, ny), jnp.float32)
    strip = 32
    for z in range(planes):
        for x in range(0, nx, strip):
            total = None
            for t in range(src_ref.shape[1]):
                term = src_ref[0, t, z, x : x + strip].astype(jnp.float32) * rec_ref[0, t, z, x : x + strip].astype(jnp.float32)
                total = term if total is None else total + term
            wide_ref[pl.ds(edge + z + x * planes, strip, stride=planes), :] = total
    rows = out_ref.shape[3]
    step = rows - 2 * edge
    for d in range(out_ref.shape[0]):
        out_ref[d, 0, 0] = wide_ref[d * step : d * step + rows, :].astype(out_ref.dtype)

def cross_pieces(source, receiver, targets):
    shots, steps, planes, nx, ny = source.shape
    halves = 2
    p = planes // halves
    rows = (nx // targets + 4) * p
    spec = pl.BlockSpec((1, steps, p, nx, ny), lambda s, h: (s, 0, h, 0, 0))
    return pl.pallas_call(
        cross_kernel,
        grid=(shots, halves),
        in_specs=[spec, spec],
        out_specs=pl.BlockSpec((targets, 1, 1, rows, ny), lambda s, h: (0, h, s, 0, 0)),
        out_shape=jax.ShapeDtypeStruct((targets, halves, shots, rows, ny), jnp.bfloat16),
        scratch_shapes=[pltpu.VMEM(((nx + 4) * p, ny), jnp.float32)],
        compiler_params=pltpu.CompilerParams(vmem_limit_bytes=48 << 20),
        name="cross",
    )(source, receiver)


def prepare_kernel(place, group_ref, w1_ref, b1_ref, w2_ref, b2_ref, k1_ref, k2_ref, bias_ref):
    co, ci = w1_ref.shape[1:]
    shots = group_ref.shape[0] // 4
    i = place()[0]
    w = k1_ref.shape[1]
    r = lax.broadcasted_iota(jnp.int32, (ci, w), 0)
    c = lax.broadcasted_iota(jnp.int32, (ci, w), 1)
    label = jnp.full((ci, w), -1, jnp.int32)
    for k in range(4):
        for s in range(shots):
            label = jnp.where(c % SC == k * shots + s, group_ref[(i ^ k) * shots + s], label)
    hit = r == label
    k2_ref[...] = jnp.zeros(k2_ref.shape, k2_ref.dtype)
    for oz in range(2):
        acc = jnp.zeros((3 * co, w), jnp.float32)
        for t in range(9):
            column = 3 * oz + t
            pick = jnp.where(hit & (c // SC == column), 1.0, 0.0).astype(jnp.bfloat16)
            left = jnp.concatenate([w1_ref[3 * t + dy] for dy in range(3)], axis=0)
            acc = acc + jnp.dot(left, pick, preferred_element_type=jnp.float32)
            for dy in range(3):
                row = (3 * oz + dy) * co
                k2_ref[row : row + co, column * co : (column + 1) * co] = w2_ref[3 * t + dy]
        k1_ref[3 * oz * co : 3 * (oz + 1) * co, :] = acc.astype(jnp.bfloat16)
    eye = lax.broadcasted_iota(jnp.int32, (co, co), 0) == lax.broadcasted_iota(jnp.int32, (co, co), 1)
    for n, b in enumerate((b1_ref, b2_ref)):
        col = jnp.sum(jnp.where(eye, jnp.broadcast_to(b[...], (co, co)), 0.0), axis=1, keepdims=True)
        bias_ref[n] = jnp.broadcast_to(col, bias_ref.shape[1:])

def prepare(place, shot_group, w1, b1, w2, b2, ny):
    co, ci = w1.shape[:2]
    w1t = w1.transpose(2, 3, 4, 0, 1).reshape(27, co, ci)
    w2t = w2.transpose(2, 3, 4, 0, 1).reshape(27, co, co)
    vmem = pl.BlockSpec(memory_space=pltpu.VMEM)
    return pl.pallas_call(
        functools.partial(prepare_kernel, place),
        in_specs=[pl.BlockSpec(memory_space=pltpu.SMEM)] + [vmem] * 4,
        out_specs=[vmem] * 3,
        out_shape=[
            jax.ShapeDtypeStruct((6 * co, 12 * SC), jnp.bfloat16),
            jax.ShapeDtypeStruct((6 * co, 12 * co), jnp.bfloat16),
            jax.ShapeDtypeStruct((2, co, ny), jnp.float32),
        ],
        name="prepare",
    )(shot_group, w1t, b1.reshape(1, co), w2t, b2.reshape(1, co))

def spread(part_ref, oz, x, bias):
    co, ny = bias.shape
    at = slice(x * ny, (x + 1) * ny)
    low_at, mid_at, high_at = (slice((3 * oz + n) * co, (3 * oz + n + 1) * co) for n in range(3))
    lane = lax.broadcasted_iota(jnp.int32, (co, ny), 1)
    low = jnp.where(lane == 0, 0.0, pltpu.roll(part_ref[low_at, at], 1, 1))
    high = jnp.where(lane == ny - 1, 0.0, pltpu.roll(part_ref[high_at, at], ny - 1, 1))
    return jnp.maximum(part_ref[mid_at, at] + low + high + bias, 0.0)

def multiply(k_ref, v_ref, z, columns, part_ref):
    ny = v_ref.shape[-1]
    for x in range(0, columns, 2):
        right = jnp.concatenate(
            [jnp.concatenate([v_ref[z + dz, x + q + dx] for dz in range(4) for dx in range(3)], axis=0) for q in range(2)], axis=1)
        part_ref[:, x * ny : (x + 2) * ny] = jnp.dot(k_ref[...], right, preferred_element_type=jnp.float32)

def conv_kernel(place, base, first, second, last, group_ref, *refs):
    early = () if first else refs[:4]
    refs = refs if first else refs[4:]
    late, (k1_ref, k2_ref, bias_ref), refs = refs[:4], refs[4:7], refs[7:]
    refs = refs if first else refs[1:]
    (out_hbm, out_ref, x_ref, h_ref, gather_ref, a0, a1, b0, b1, t0, t1, sems) = refs
    ny = x_ref.shape[-1]
    nhx = h_ref.shape[1]
    co, zs, nox = out_ref.shape[:3]
    shots, rows = late[0].shape[1:3]
    per = 2
    i, ni, j, nj = place()
    parts1, parts2, turns = (a0, a1), (b0, b1), (t0, t1)
    skip = 0 if first else per

    def lay(l):
        if isinstance(l, int) and l < skip:
            source, nh = early, early[0].shape[0]
            want = l + nh - skip
            if second:
                want = want - jnp.where(i == 0, 1, 0)
        else:
            source, nh = late, late[0].shape[0]
            want = l - skip
            if first:
                want = want - jnp.where(i == 0, 1, 0)
            if last:
                want = want + jnp.where(i == ni - 1, 1, 0)
        here = jnp.clip(want, 0, nh - 1)
        keep = jnp.where(want == here, 1.0, 0.0)
        for k, p in enumerate(source):
            for s in range(shots):
                gather_ref[pl.ds(k * shots + s, rows, stride=SC), :] = p[here, s].astype(jnp.float32) * keep
        for x in range(rows // per):
            for z in range(per):
                at = (x * per + z) * SC
                x_ref[l * per + z, x] = gather_ref[at : at + SC, :].astype(jnp.bfloat16)

    def hide(pair, part_ref, lives):
        for oz in range(2):
            for x in range(nhx):
                v = spread(part_ref, oz, x, bias_ref[0])
                keep = lives[oz]
                if x == 0:
                    keep = keep & (j > 0)
                if x == nhx - 1:
                    keep = keep & (j < nj - 1)
                h_ref[2 * pair + oz, x] = jnp.where(keep, v, 0.0).astype(h_ref.dtype)

    def emit(pair, part_ref):
        for oz in range(2):
            turn_ref = turns[oz]
            for x in range(nox):
                turn_ref[pl.ds(x, co, stride=nox), :] = spread(part_ref, oz, x, bias_ref[1])
            out_ref[:, 2 * pair + oz] = turn_ref[...].reshape(co, nox, ny).astype(out_ref.dtype)

    gather_ref[...] = jnp.zeros(gather_ref.shape, jnp.float32)
    ahead = 5
    for l in range(ahead):
        lay(l)
    always = i >= 0
    for pair in range(2):
        multiply(k1_ref, x_ref, 2 * pair, nhx, parts1[pair])
        hide(pair, parts1[pair], ((i > 0) if first and pair == 0 else always, always))
    multiply(k1_ref, x_ref, 4, nhx, a1)

    @pl.when(group_ref[0] < 0)
    def _():
        for n in range(2):
            out_ref[n, 0] = parts1[n][0:nox, 0:ny].astype(out_ref.dtype)
            out_ref[n, 1] = parts2[n][0:nox, 0:ny].astype(out_ref.dtype)
            out_ref[n, 2] = turns[n][0:nox, :].astype(out_ref.dtype)
        out_ref[2, 0] = h_ref[-group_ref[0], 0, 0:nox, :]
        out_ref[3, 0] = x_ref[-group_ref[0], 0, 0:nox, :]

    def quad(n, final=False):
        for u in range(2):
            p = 2 * n + u
            multiply(k2_ref, h_ref, 2 * p, nox, parts2[u])
            if not final:
                multiply(k1_ref, x_ref, 2 * p + 6, nhx, parts1[u])
            if not (final and u):
                hide(p + 2, parts1[1 - u], (always, ((2 * p + 5 != zs + 1) | (i < ni - 1)) if last else always))
            emit(jnp.maximum(p - 1, 0), parts2[1 - u])
            if not final:
                lay(p + ahead)

    quads = zs // 4
    cut = quads - 1
    ready = 2 * (2 * cut - 1)
    pl.loop(0, cut)(quad)
    head = pltpu.make_async_copy(out_ref.at[:, :ready], out_hbm.at[:, base : base + ready], sems.at[0])
    head.start()
    quad(cut, True)
    emit(zs // 2 - 1, parts2[1])
    tail = pltpu.make_async_copy(out_ref.at[:, ready:], out_hbm.at[:, base + ready : base + zs], sems.at[1])
    tail.start()
    head.wait()
    tail.wait()


def convolutions(place, shot_group, early, late, done, weights, base, out_rows, second, last):
    first = early is None
    shots, rows, ny = late[0].shape[1:]
    halves = late[0].shape[0] + (0 if first else 2)
    nz = halves * 2 - 4
    nx = rows // 2 - 4
    k1, k2, bias = weights
    co = bias.shape[1]
    vmem = pl.BlockSpec(memory_space=pltpu.VMEM)
    hbm = pl.BlockSpec(memory_space=pl.ANY)
    f32 = jnp.float32
    pieces = list(late) if first else list(early) + list(late)
    more = [] if first else [done]
    return pl.pallas_call(
        functools.partial(conv_kernel, place, base, first, second, last),
        in_specs=[pl.BlockSpec(memory_space=pltpu.SMEM)] + [vmem] * (len(pieces) + 3) + [hbm] * len(more),
        out_specs=hbm,
        out_shape=jax.ShapeDtypeStruct((co, out_rows, nx, ny), jnp.bfloat16),
        scratch_shapes=[
            pltpu.VMEM((co, nz, nx, ny), jnp.bfloat16),
            pltpu.VMEM((nz + 10, nx + 4, SC, ny), jnp.bfloat16),
            pltpu.VMEM((nz + 4, nx + 2, co, ny), jnp.bfloat16),
            pltpu.VMEM((rows * SC, ny), f32),
            pltpu.VMEM((6 * co, (nx + 2) * ny), f32),
            pltpu.VMEM((6 * co, (nx + 2) * ny), f32),
            pltpu.VMEM((6 * co, nx * ny), f32),
            pltpu.VMEM((6 * co, nx * ny), f32),
            pltpu.VMEM((nx * co, ny), f32),
            pltpu.VMEM((nx * co, ny), f32),
            pltpu.SemaphoreType.DMA((2,)),
        ],
        input_output_aliases={} if first else {4 + len(pieces): 0},
        compiler_params=pltpu.CompilerParams(vmem_limit_bytes=20 << 20),
        name="head" if first else "tail" if last else "middle",
    )(shot_group, *pieces, k1, k2, bias, *more)


def shards(source, receiver, shot_group, w1, b1, w2, b2):
    ni, nj = lax.axis_size("shot"), lax.axis_size("slab")
    i = lax.axis_index("shot")
    place = lambda: (lax.axis_index("shot"), ni, lax.axis_index("slab"), nj)
    weights = prepare(place, shot_group, w1, b1, w2, b2, source.shape[-1])
    pieces = cross_pieces(source, receiver, nj)
    swapped = lax.all_to_all(pieces, "slab", 0, 0, tiled=True)
    swapped, weights = lax.optimization_barrier((swapped, weights))
    halves = swapped.reshape((-1,) + swapped.shape[2:])
    span = halves.shape[0] // ni
    rows = source.shape[2] * nj // ni
    sizes = (span // 2 + 2, span // 2)
    chunks, at = [], -1
    for size in sizes:
        here = []
        for k in range(ni):
            start = jnp.clip((i ^ k) * span + at, 0, halves.shape[0] - size)
            part = lax.dynamic_slice_in_dim(halves, start, size, 0)
            here.append(part if k == 0 else lax.ppermute(part, "shot", [(a, a ^ k) for a in range(ni)]))
        chunks.append(here)
        at += size
    result, base = None, 0
    for c, size in enumerate(sizes):
        result = convolutions(
            place, shot_group, chunks[c - 1] if c else None, chunks[c], result, weights,
            base, rows, c == 1, c == len(sizes) - 1)
        base += 2 * size - (0 if c else 4)
    return result


def solution(mesh):
    fields = P("shot", None, "slab", None, None)
    return jax.shard_map(
        shards, mesh=mesh, in_specs=(fields, fields, P(), P(), P(), P(), P()),
        out_specs=P(None, "shot", "slab", None), check_vma=False)
```

```python
import functools

import jax
import jax.numpy as jnp
from jax import lax
from jax.experimental import pallas as pl
from jax.experimental.pallas import tpu as pltpu
from jax.sharding import PartitionSpec as P

SC = 16

def cross_kernel(src_ref, rec_ref, out_ref, wide_ref):
    planes, nx, ny = src_ref.shape[2:]
    first = (pl.program_id(0) == 0) & (pl.program_id(1) == 0)
    edge = 2 * planes
    @pl.when(first)
    def _():
        wide_ref[0:edge, :] = jnp.zeros((edge, ny), jnp.float32)
        wide_ref[edge + planes * nx :, :] = jnp.zeros((edge, ny), jnp.float32)
    strip = 32
    for z in range(planes):
        for x in range(0, nx, strip):
            total = None
            for t in range(src_ref.shape[1]):
                term = src_ref[0, t, z, x : x + strip].astype(jnp.float32) * rec_ref[0, t, z, x : x + strip].astype(jnp.float32)
                total = term if total is None else total + term
            wide_ref[pl.ds(edge + z + x * planes, strip, stride=planes), :] = total
    rows = out_ref.shape[3]
    step = rows - 2 * edge
    for d in range(out_ref.shape[0]):
        out_ref[d, 0, 0] = wide_ref[d * step : d * step + rows, :].astype(out_ref.dtype)

def cross_pieces(source, receiver, targets):
    shots, steps, planes, nx, ny = source.shape
    halves = 2
    p = planes // halves
    rows = (nx // targets + 4) * p
    spec = pl.BlockSpec((1, steps, p, nx, ny), lambda s, h: (s, 0, h, 0, 0))
    return pl.pallas_call(
        cross_kernel,
        grid=(shots, halves),
        in_specs=[spec, spec],
        out_specs=pl.BlockSpec((targets, 1, 1, rows, ny), lambda s, h: (0, h, s, 0, 0)),
        out_shape=jax.ShapeDtypeStruct((targets, halves, shots, rows, ny), jnp.bfloat16),
        scratch_shapes=[pltpu.VMEM(((nx + 4) * p, ny), jnp.float32)],
        compiler_params=pltpu.CompilerParams(vmem_limit_bytes=48 << 20),
        name="cross",
    )(source, receiver)


def prepare_kernel(place, group_ref, w1_ref, b1_ref, w2_ref, b2_ref, k1_ref, k2_ref, bias_ref):
    co, ci = w1_ref.shape[1:]
    shots = group_ref.shape[0] // 4
    i = place()[0]
    w = k1_ref.shape[1]
    r = lax.broadcasted_iota(jnp.int32, (ci, w), 0)
    c = lax.broadcasted_iota(jnp.int32, (ci, w), 1)
    label = jnp.full((ci, w), -1, jnp.int32)
    for k in range(4):
        for s in range(shots):
            label = jnp.where(c % SC == k * shots + s, group_ref[(i ^ k) * shots + s], label)
    hit = r == label
    k2_ref[...] = jnp.zeros(k2_ref.shape, k2_ref.dtype)
    for oz in range(2):
        acc = jnp.zeros((3 * co, w), jnp.float32)
        for t in range(9):
            column = 3 * oz + t
            pick = jnp.where(hit & (c // SC == column), 1.0, 0.0).astype(jnp.bfloat16)
            left = jnp.concatenate([w1_ref[3 * t + dy] for dy in range(3)], axis=0)
            acc = acc + jnp.dot(left, pick, preferred_element_type=jnp.float32)
            for dy in range(3):
                row = (3 * oz + dy) * co
                k2_ref[row : row + co, column * co : (column + 1) * co] = w2_ref[3 * t + dy]
        k1_ref[3 * oz * co : 3 * (oz + 1) * co, :] = acc.astype(jnp.bfloat16)
    eye = lax.broadcasted_iota(jnp.int32, (co, co), 0) == lax.broadcasted_iota(jnp.int32, (co, co), 1)
    for n, b in enumerate((b1_ref, b2_ref)):
        col = jnp.sum(jnp.where(eye, jnp.broadcast_to(b[...], (co, co)), 0.0), axis=1, keepdims=True)
        bias_ref[n] = jnp.broadcast_to(col, bias_ref.shape[1:])

def prepare(place, shot_group, w1, b1, w2, b2, ny):
    co, ci = w1.shape[:2]
    w1t = w1.transpose(2, 3, 4, 0, 1).reshape(27, co, ci)
    w2t = w2.transpose(2, 3, 4, 0, 1).reshape(27, co, co)
    vmem = pl.BlockSpec(memory_space=pltpu.VMEM)
    return pl.pallas_call(
        functools.partial(prepare_kernel, place),
        in_specs=[pl.BlockSpec(memory_space=pltpu.SMEM)] + [vmem] * 4,
        out_specs=[vmem] * 3,
        out_shape=[
            jax.ShapeDtypeStruct((6 * co, 12 * SC), jnp.bfloat16),
            jax.ShapeDtypeStruct((6 * co, 12 * co), jnp.bfloat16),
            jax.ShapeDtypeStruct((2, co, ny), jnp.float32),
        ],
        name="prepare",
    )(shot_group, w1t, b1.reshape(1, co), w2t, b2.reshape(1, co))

def spread(part_ref, oz, x, bias):
    co, ny = bias.shape
    at = slice(x * ny, (x + 1) * ny)
    low_at, mid_at, high_at = (slice((3 * oz + n) * co, (3 * oz + n + 1) * co) for n in range(3))
    lane = lax.broadcasted_iota(jnp.int32, (co, ny), 1)
    low = jnp.where(lane == 0, 0.0, pltpu.roll(part_ref[low_at, at], 1, 1))
    high = jnp.where(lane == ny - 1, 0.0, pltpu.roll(part_ref[high_at, at], ny - 1, 1))
    return jnp.maximum(part_ref[mid_at, at] + low + high + bias, 0.0)

def multiply(k_ref, v_ref, z, columns, part_ref):
    ny = v_ref.shape[-1]
    for x in range(0, columns, 2):
        right = jnp.concatenate(
            [jnp.concatenate([v_ref[z + dz, x + q + dx] for dz in range(4) for dx in range(3)], axis=0) for q in range(2)], axis=1)
        part_ref[:, x * ny : (x + 2) * ny] = jnp.dot(k_ref[...], right, preferred_element_type=jnp.float32)

def conv_kernel(place, base, first, second, last, group_ref, *refs):
    early = () if first else refs[:4]
    refs = refs if first else refs[4:]
    late, (k1_ref, k2_ref, bias_ref), refs = refs[:4], refs[4:7], refs[7:]
    refs = refs if first else refs[1:]
    (out_hbm, out_ref, x_ref, h_ref, gather_ref, a0, a1, b0, b1, t0, t1, sems) = refs
    ny = x_ref.shape[-1]
    nhx = h_ref.shape[1]
    co, zs, nox = out_ref.shape[:3]
    shots, rows = late[0].shape[1:3]
    per = 2
    i, ni, j, nj = place()
    parts1, parts2, turns = (a0, a1), (b0, b1), (t0, t1)
    skip = 0 if first else per

    def lay(l):
        if isinstance(l, int) and l < skip:
            source, nh = early, early[0].shape[0]
            want = l + nh - skip
            if second:
                want = want - jnp.where(i == 0, 1, 0)
        else:
            source, nh = late, late[0].shape[0]
            want = l - skip
            if first:
                want = want - jnp.where(i == 0, 1, 0)
            if last:
                want = want + jnp.where(i == ni - 1, 1, 0)
        here = jnp.clip(want, 0, nh - 1)
        keep = jnp.where(want == here, 1.0, 0.0)
        for k, p in enumerate(source):
            for s in range(shots):
                gather_ref[pl.ds(k * shots + s, rows, stride=SC), :] = p[here, s].astype(jnp.float32) * keep
        for x in range(rows // per):
            for z in range(per):
                at = (x * per + z) * SC
                x_ref[l * per + z, x] = gather_ref[at : at + SC, :].astype(jnp.bfloat16)

    def hide(pair, part_ref, lives):
        for oz in range(2):
            for x in range(nhx):
                v = spread(part_ref, oz, x, bias_ref[0])
                keep = lives[oz]
                if x == 0:
                    keep = keep & (j > 0)
                if x == nhx - 1:
                    keep = keep & (j < nj - 1)
                h_ref[2 * pair + oz, x] = jnp.where(keep, v, 0.0).astype(h_ref.dtype)

    def emit(pair, part_ref):
        for oz in range(2):
            turn_ref = turns[oz]
            for x in range(nox):
                turn_ref[pl.ds(x, co, stride=nox), :] = spread(part_ref, oz, x, bias_ref[1])
            out_ref[:, 2 * pair + oz] = turn_ref[...].reshape(co, nox, ny).astype(out_ref.dtype)

    gather_ref[...] = jnp.zeros(gather_ref.shape, jnp.float32)
    ahead = 5
    always = i >= 0
    lay(0)
    lay(1)
    multiply(k1_ref, x_ref, 0, nhx, a0)
    lay(2)
    multiply(k1_ref, x_ref, 2, nhx, a1)
    hide(0, a0, ((i > 0) if first else always, always))
    lay(3)
    lay(4)
    hide(1, a1, (always, always))
    multiply(k1_ref, x_ref, 4, nhx, a1)

    @pl.when(group_ref[0] < 0)
    def _():
        for n in range(2):
            out_ref[n, 0] = parts1[n][0:nox, 0:ny].astype(out_ref.dtype)
            out_ref[n, 1] = parts2[n][0:nox, 0:ny].astype(out_ref.dtype)
            out_ref[n, 2] = turns[n][0:nox, :].astype(out_ref.dtype)
        out_ref[2, 0] = h_ref[-group_ref[0], 0, 0:nox, :]
        out_ref[3, 0] = x_ref[-group_ref[0], 0, 0:nox, :]

    def quad(n, final=False):
        for u in range(2):
            p = 2 * n + u
            multiply(k2_ref, h_ref, 2 * p, nox, parts2[u])
            if not final:
                multiply(k1_ref, x_ref, 2 * p + 6, nhx, parts1[u])
            if not (final and u):
                hide(p + 2, parts1[1 - u], (always, ((2 * p + 5 != zs + 1) | (i < ni - 1)) if last else always))
            emit(jnp.maximum(p - 1, 0), parts2[1 - u])
            if not final:
                lay(p + ahead)

    quads = zs // 4
    cut = quads - 1
    ready = 2 * (2 * cut - 1)
    pl.loop(0, cut)(quad)
    head = pltpu.make_async_copy(out_ref.at[:, :ready], out_hbm.at[:, base : base + ready], sems.at[0])
    head.start()
    quad(cut, True)
    body = pltpu.make_async_copy(out_ref.at[:, ready : zs - 2], out_hbm.at[:, base + ready : base + zs - 2], sems.at[1])
    body.start()
    emit(zs // 2 - 1, parts2[1])
    tail = pltpu.make_async_copy(out_ref.at[:, zs - 2 :], out_hbm.at[:, base + zs - 2 : base + zs], sems.at[2])
    tail.start()
    head.wait()
    body.wait()
    tail.wait()


def convolutions(place, shot_group, early, late, done, weights, base, out_rows, second, last):
    first = early is None
    shots, rows, ny = late[0].shape[1:]
    halves = late[0].shape[0] + (0 if first else 2)
    nz = halves * 2 - 4
    nx = rows // 2 - 4
    k1, k2, bias = weights
    co = bias.shape[1]
    vmem = pl.BlockSpec(memory_space=pltpu.VMEM)
    hbm = pl.BlockSpec(memory_space=pl.ANY)
    f32 = jnp.float32
    pieces = list(late) if first else list(early) + list(late)
    more = [] if first else [done]
    return pl.pallas_call(
        functools.partial(conv_kernel, place, base, first, second, last),
        in_specs=[pl.BlockSpec(memory_space=pltpu.SMEM)] + [vmem] * (len(pieces) + 3) + [hbm] * len(more),
        out_specs=hbm,
        out_shape=jax.ShapeDtypeStruct((co, out_rows, nx, ny), jnp.bfloat16),
        scratch_shapes=[
            pltpu.VMEM((co, nz, nx, ny), jnp.bfloat16),
            pltpu.VMEM((nz + 10, nx + 4, SC, ny), jnp.bfloat16),
            pltpu.VMEM((nz + 4, nx + 2, co, ny), jnp.bfloat16),
            pltpu.VMEM((rows * SC, ny), f32),
            pltpu.VMEM((6 * co, (nx + 2) * ny), f32),
            pltpu.VMEM((6 * co, (nx + 2) * ny), f32),
            pltpu.VMEM((6 * co, nx * ny), f32),
            pltpu.VMEM((6 * co, nx * ny), f32),
            pltpu.VMEM((nx * co, ny), f32),
            pltpu.VMEM((nx * co, ny), f32),
            pltpu.SemaphoreType.DMA((3,)),
        ],
        input_output_aliases={} if first else {4 + len(pieces): 0},
        compiler_params=pltpu.CompilerParams(vmem_limit_bytes=20 << 20),
        name="head" if first else "tail" if last else "middle",
    )(shot_group, *pieces, k1, k2, bias, *more)


def shards(source, receiver, shot_group, w1, b1, w2, b2):
    ni, nj = lax.axis_size("shot"), lax.axis_size("slab")
    i = lax.axis_index("shot")
    place = lambda: (lax.axis_index("shot"), ni, lax.axis_index("slab"), nj)
    weights = prepare(place, shot_group, w1, b1, w2, b2, source.shape[-1])
    pieces = cross_pieces(source, receiver, nj)
    swapped = lax.all_to_all(pieces, "slab", 0, 0, tiled=True)
    swapped, weights = lax.optimization_barrier((swapped, weights))
    halves = swapped.reshape((-1,) + swapped.shape[2:])
    span = halves.shape[0] // ni
    rows = source.shape[2] * nj // ni
    sizes = (span // 2 + 2, span // 2)
    chunks, at = [], -1
    for size in sizes:
        here = []
        for k in range(ni):
            start = jnp.clip((i ^ k) * span + at, 0, halves.shape[0] - size)
            part = lax.dynamic_slice_in_dim(halves, start, size, 0)
            here.append(part if k == 0 else lax.ppermute(part, "shot", [(a, a ^ k) for a in range(ni)]))
        chunks.append(here)
        at += size
    result, base = None, 0
    for c, size in enumerate(sizes):
        result = convolutions(
            place, shot_group, chunks[c - 1] if c else None, chunks[c], result, weights,
            base, rows, c == 1, c == len(sizes) - 1)
        base += 2 * size - (0 if c else 4)
    return result


def solution(mesh):
    fields = P("shot", None, "slab", None, None)
    return jax.shard_map(
        shards, mesh=mesh, in_specs=(fields, fields, P(), P(), P(), P(), P()),
        out_specs=P(None, "shot", "slab", None), check_vma=False)
```
